512 devices in a mesh: alpha: 16 (over z_hi, x, core), beta: 32 (over y, z_lo).
Axes of the slice: x: 4, y: 4, z: 16 (z_hi: 2, z_lo: 8; z = z_hi * 8 + z_lo), core: 2. Of those that a mesh axis runs over, the one named last changes fastest.
Arguments:
- coefficients: float32 [6144, 12288], P('alpha', 'beta'), may hold values from -6 to 6
- alpha_coupling: float32 [2, 6144, 384], P(None, 'alpha'), may hold values from -0.125 to 0.125
- beta_coupling: float32 [3, 12288, 384], P(None, 'beta'), may hold values from -0.125 to 0.125
- alpha_energy: float32 [6144], P('alpha'), may hold values from -0.8 to 0.8
- beta_energy: float32 [12288], P('beta'), may hold values from -0.8 to 0.8
- alpha_bits: int32 [4], replicated, may hold values from 0 to 3, each once
- beta_bits: int32 [5], replicated, may hold values from 0 to 4, each once
- alpha_mask: int32 [16, 2], P('alpha'), may hold values 0 or 1
- beta_mask: int32 [32, 3], P('beta'), may hold values 0 or 1
Outputs:
- sigma_vector: float32 [6144, 12288], P('alpha', 'beta')
- sigma_squared: float32 [6144, 12288], P('alpha', 'beta')
The draws below stay inside these ranges and needn't reach their ends.
Inputs may be any that keep to these rules, and one draw needn't show every extreme that they name: Slot k of the alpha lists, k < 2, couples block a with block a XOR 2^alpha_bits[k]; the remaining entries are unused. Slot k of the beta lists, k < 3, couples block b with block b XOR 2^beta_bits[k]; the remaining entries are unused.
All inputs are finite; a program needn't handle non-finite values. No bound on the sum of `alpha_mask` or of `beta_mask` on one device may be relied on, other than what follows from the above.
Results may differ from the reference program's by a relative error of at most 0.0001.
Values sent between devices are 32-bit elements; how exact they have to be, the bound alone decides.
No kernel may reach another device: no remote copies, remote signals or barrier semaphores. Data moves between devices by JAX's collectives and lax.ppermute only.
A program may use at most 64 MiB of HBM per device.

```python
import jax
import jax.numpy as jnp
from jax import lax

BLOCK = 384
ALPHA_SLOTS = 2
BETA_SLOTS = 3
ALPHA_BLOCKS = 16
BETA_BLOCKS = 32
ALPHA_LEVELS = 4
BETA_LEVELS = 5
ALPHA_STRINGS = 6144
BETA_STRINGS = 12288


def set_ends(values, stream_key, low, high):
    dims = values.shape
    place = [jax.random.randint(jax.random.fold_in(stream_key, axis), (), 0, dims[axis]) for axis in range(len(dims))]
    values = values.at[tuple(place)].set(low)
    longest = dims.index(max(dims))
    place[longest] = (place[longest] + 1) % dims[longest]
    return values.at[tuple(place)].set(high)


def steps_of(rng, shape, split, low, largest):
    gain, own = 1.0, jax.random.fold_in(rng, 6)
    for dim, parts in split:
        steps = jnp.exp(jax.random.uniform(jax.random.fold_in(own, dim), (parts,), jnp.float32, low / len(split), largest / len(split)))
        gain = gain * jnp.repeat(steps, shape[dim] // parts).reshape([-1 if axis == dim else 1 for axis in range(len(shape))])
    return gain


def noise(key, extent, width, reach, split=(), kind=jnp.bfloat16):
    drawn = width * jax.random.normal(key, extent, jnp.float32)
    if split:
        drawn = drawn * steps_of(key, extent, split, -0.22, 0.18)
    return jnp.clip(drawn, -reach, reach).astype(kind)


def setup_inputs(seed: int = 0) -> dict:
    splits = jax.random.split(jax.random.key(seed), 10)
    return {
        "coefficients": noise(splits[0], (ALPHA_STRINGS, BETA_STRINGS), 1.0, 6.0, ((0, 16), (1, 32)), jnp.float32),
        "alpha_coupling": noise(splits[1], (ALPHA_SLOTS, ALPHA_STRINGS, BLOCK), ((ALPHA_SLOTS + BETA_SLOTS) * BLOCK) ** -0.5, 0.125, ((1, 16),), jnp.float32),
        "beta_coupling": noise(splits[2], (BETA_SLOTS, BETA_STRINGS, BLOCK), ((ALPHA_SLOTS + BETA_SLOTS) * BLOCK) ** -0.5, 0.125, ((1, 32),), jnp.float32),
        "alpha_energy": jnp.clip(jax.random.uniform(splits[3], (ALPHA_STRINGS,), jnp.float32, -0.8, 0.8) * steps_of(splits[3], (ALPHA_STRINGS,), ((0, 16),), -0.4, 0.0), -0.8, 0.8),
        "beta_energy": jnp.clip(jax.random.uniform(splits[4], (BETA_STRINGS,), jnp.float32, -0.8, 0.8) * steps_of(splits[4], (BETA_STRINGS,), ((0, 32),), -0.4, 0.0), -0.8, 0.8),
        "alpha_bits": jax.random.permutation(splits[5], ALPHA_LEVELS).astype(jnp.int32),
        "beta_bits": jax.random.permutation(splits[6], BETA_LEVELS).astype(jnp.int32),
        "alpha_mask": set_ends((jax.random.randint(splits[7], (ALPHA_BLOCKS, ALPHA_SLOTS), 0, 4) < 3).astype(jnp.int32), jax.random.fold_in(splits[7], 1), 0, 1),
        "beta_mask": set_ends((jax.random.randint(splits[8], (BETA_BLOCKS, BETA_SLOTS), 0, 4) < 3).astype(jnp.int32), jax.random.fold_in(splits[8], 1), 0, 1),
    }


def apply_operator(vector, alpha_coupling, beta_coupling, diagonal, alpha_bits, beta_bits, alpha_mask, beta_mask):
    alpha_blocks = alpha_mask.shape[0]
    beta_blocks = beta_mask.shape[0]
    block = alpha_coupling.shape[2]
    result = diagonal * vector
    alpha_index = jnp.arange(alpha_blocks, dtype=jnp.int32)
    beta_index = jnp.arange(beta_blocks, dtype=jnp.int32)
    blocked = vector.reshape(alpha_blocks, block, vector.shape[1])
    for position in range(alpha_mask.shape[1]):
        partner = jnp.bitwise_xor(alpha_index, jnp.left_shift(jnp.int32(1), alpha_bits[position].astype(jnp.int32)))
        moved = blocked[partner]
        rows = alpha_coupling[position].reshape(alpha_blocks, block, block)
        term = jnp.einsum("aij,ajc->aic", rows, moved, precision=lax.Precision.HIGHEST)
        weight = alpha_mask[:, position].astype(jnp.float32)
        result = result + (weight[:, None, None] * term).reshape(vector.shape)
    columns = vector.reshape(vector.shape[0], beta_blocks, block)
    for position in range(beta_mask.shape[1]):
        partner = jnp.bitwise_xor(beta_index, jnp.left_shift(jnp.int32(1), beta_bits[position].astype(jnp.int32)))
        moved = columns[:, partner, :]
        rows = beta_coupling[position].reshape(beta_blocks, block, block)
        term = jnp.einsum("xbj,bij->xbi", moved, rows, precision=lax.Precision.HIGHEST)
        weight = beta_mask[:, position].astype(jnp.float32)
        result = result + (term * weight[None, :, None]).reshape(vector.shape)
    return result


def reference(coefficients, alpha_coupling, beta_coupling, alpha_energy, beta_energy, alpha_bits, beta_bits, alpha_mask, beta_mask):
    diagonal = alpha_energy[:, None] + beta_energy[None, :]
    sigma_vector = apply_operator(coefficients, alpha_coupling, beta_coupling, diagonal, alpha_bits, beta_bits, alpha_mask, beta_mask)
    sigma_squared = apply_operator(sigma_vector, alpha_coupling, beta_coupling, diagonal, alpha_bits, beta_bits, alpha_mask, beta_mask)
    return (sigma_vector, sigma_squared)
```

```python
import itertools

import jax
import jax.numpy as jnp
from jax import lax
from jax.sharding import PartitionSpec as P


def swapped(value, axis, stride):
    mask = 2**stride
    pairs = [(source, source ^ mask) for source in range(lax.axis_size(axis))]
    return lax.ppermute(value, axis, pairs)


def levels(axis):
    return lax.axis_size(axis).bit_length() - 1


def chosen(bits, slots, count):
    sets = list(itertools.combinations(range(count), slots))
    used = jnp.stack([bits[k] for k in range(slots)])
    key = jnp.sum(jnp.left_shift(jnp.int32(1), used))
    table = jnp.array([sum(1 << b for b in s) for s in sets], jnp.int32)
    which = jnp.sum(jnp.where(table == key, jnp.arange(len(sets), dtype=jnp.int32), 0))
    rank = jnp.sum((used[None, :] < used[:, None]).astype(jnp.int32), axis=1)
    order = [jnp.sum(jnp.where(rank == r, jnp.arange(slots, dtype=jnp.int32), 0)) for r in range(slots)]
    return sets, which, order


def per_device(
    coefficients,
    alpha_coupling,
    beta_coupling,
    alpha_energy,
    beta_energy,
    alpha_bits,
    beta_bits,
    alpha_mask,
    beta_mask,
):
    alpha_slots = alpha_coupling.shape[0]
    beta_slots = beta_coupling.shape[0]
    alpha_sets, alpha_which, alpha_order = chosen(alpha_bits, alpha_slots, levels("alpha"))
    beta_sets, beta_which, beta_order = chosen(beta_bits, beta_slots, levels("beta"))
    which = alpha_which * len(beta_sets) + beta_which
    diagonal = alpha_energy[:, None] + beta_energy[None, :]

    def exchange(alpha_set, beta_set):
        def run(tile):
            return tuple([swapped(tile, "alpha", b) for b in alpha_set] + [swapped(tile, "beta", b) for b in beta_set])

        return run

    branches = [exchange(a, b) for a in alpha_sets for b in beta_sets]

    def apply_operator(tile):
        tiles = lax.switch(which, branches, tile)
        result = diagonal * tile
        for place in range(alpha_slots):
            slot = alpha_order[place]
            matrix = lax.dynamic_index_in_dim(alpha_coupling, slot, 0, keepdims=False)
            product = jnp.dot(
                matrix,
                tiles[place],
                precision=lax.Precision.HIGH,
                preferred_element_type=jnp.float32,
            )
            result = result + alpha_mask[0, slot].astype(jnp.float32) * product
        for place in range(beta_slots):
            slot = beta_order[place]
            matrix = lax.dynamic_index_in_dim(beta_coupling, slot, 0, keepdims=False)
            product = lax.dot_general(
                tiles[alpha_slots + place],
                matrix,
                (((1,), (1,)), ((), ())),
                precision=lax.Precision.HIGH,
                preferred_element_type=jnp.float32,
            )
            result = result + beta_mask[0, slot].astype(jnp.float32) * product
        return result

    sigma_vector = apply_operator(coefficients)
    sigma_squared = apply_operator(sigma_vector)
    return (sigma_vector, sigma_squared)


def solution(mesh):
    return jax.shard_map(
        per_device,
        mesh=mesh,
        in_specs=(
            P("alpha", "beta"),
            P(None, "alpha", None),
            P(None, "beta", None),
            P("alpha"),
            P("beta"),
            P(),
            P(),
            P("alpha", None),
            P("beta", None),
        ),
        out_specs=(P("alpha", "beta"), P("alpha", "beta")),
        check_vma=False,
    )
```

```python
import itertools

import jax
import jax.numpy as jnp
from jax import lax
from jax.experimental import pallas as pl
from jax.experimental.pallas import tpu as pltpu
from jax.sharding import PartitionSpec as P

F32, BF16 = jnp.float32, jnp.bfloat16
RANK = {("alpha", 0): 0, ("beta", 0): 1, ("alpha", 1): 2, ("beta", 3): 3, ("alpha", 2): 4,
        ("beta", 4): 5, ("beta", 1): 6, ("beta", 2): 7, ("alpha", 3): 8}


def swapped(value, axis, stride):
    mask = 2**stride
    pairs = [(source, source ^ mask) for source in range(lax.axis_size(axis))]
    return lax.ppermute(value, axis, pairs)


def levels(axis):
    return lax.axis_size(axis).bit_length() - 1


def colex(count, slots):
    return sorted(itertools.combinations(range(count), slots), key=lambda s: s[::-1])


def plan_kernel(alpha_bits, beta_bits, plan):
    a0, a1 = alpha_bits[0], alpha_bits[1]
    low, high = jnp.minimum(a0, a1), jnp.maximum(a0, a1)
    plan[0] = (high * (high - 1)) // 2 + low
    first = (a0 > a1).astype(jnp.int32)
    plan[2] = first
    plan[3] = 1 - first
    b = [beta_bits[k] for k in range(3)]
    ranks = [sum((b[j] < b[k]).astype(jnp.int32) for j in range(3) if j != k) for k in range(3)]
    low = jnp.minimum(jnp.minimum(b[0], b[1]), b[2])
    high = jnp.maximum(jnp.maximum(b[0], b[1]), b[2])
    middle = b[0] + b[1] + b[2] - low - high
    plan[1] = (high * (high - 1) * (high - 2)) // 6 + (middle * (middle - 1)) // 2 + low
    for place in range(3):
        plan[4 + place] = sum(jnp.where(ranks[k] == place, k, 0) for k in range(3))
    plan[7] = 0


def split(value):
    high = value.astype(BF16)
    return high, (value - high.astype(F32)).astype(BF16)


def apply_kernel(alpha_slots, beta_slots, *refs):
    plan, alpha_mask, beta_mask, alpha_energy, beta_energy = refs[:5]
    sources = refs[5 : 5 + 3 + alpha_slots + beta_slots]
    out = refs[5 + len(sources)]
    buffers = refs[6 + len(sources) : 6 + 2 * len(sources)]
    sems, lhs_hi, lhs_lo, rhs_hi, rhs_lo = refs[6 + 2 * len(sources) :]
    copies = [pltpu.make_async_copy(s, d, sems.at[i]) for i, (s, d) in enumerate(zip(sources, buffers))]
    for copy in copies:
        copy.start()
    alpha_coupling, beta_coupling, tile = buffers[:3]
    alpha_tiles, beta_tiles = buffers[3 : 3 + alpha_slots], buffers[3 + alpha_slots :]
    n = tile.shape[0]

    copies[0].wait()
    for place in range(alpha_slots):
        copies[3 + place].wait()
        slot = plan[2 + place]
        at = pl.ds(place * n, n)
        matrix = alpha_coupling[slot] * alpha_mask[0, slot].astype(F32)
        lhs_hi[:, at], lhs_lo[:, at] = split(matrix)
        rhs_hi[at, :], rhs_lo[at, :] = split(alpha_tiles[place][...])
    k = alpha_slots * n

    def product(left, right):
        return lax.dot_general(left, right, (((1,), (0,)), ((), ())), preferred_element_type=F32)

    total = product(lhs_hi[:, :k], rhs_hi[...])
    total += product(lhs_hi[:, :k], rhs_lo[...])
    total += product(lhs_lo[:, :k], rhs_hi[...])

    copies[2].wait()
    rows = jnp.transpose(jnp.broadcast_to(alpha_energy[...], (128, n)))
    rows = jnp.concatenate([rows] * (n // 128), axis=1)
    out[...] = total + (rows + beta_energy[...]) * tile[...]

    copies[1].wait()

    def against(left, right):
        return lax.dot_general(left, right, (((1,), (1,)), ((), ())), preferred_element_type=F32)

    total = None
    for place in range(beta_slots):
        copies[3 + alpha_slots + place].wait()
        slot = plan[2 + alpha_slots + place]
        matrix = beta_coupling[slot] * beta_mask[0, slot].astype(F32)
        right_hi, right_lo = split(matrix)
        left_hi, left_lo = split(beta_tiles[place][...])
        part = against(left_hi, right_hi) + against(left_lo, right_hi) + against(left_hi, right_lo)
        total = part if total is None else total + part
    out[...] += total


def apply_operator(plan, alpha_mask, beta_mask, alpha_energy, beta_energy, alpha_coupling, beta_coupling, tile, tiles):
    alpha_slots, beta_slots = alpha_coupling.shape[0], beta_coupling.shape[0]
    n = tile.shape[0]
    big = [alpha_coupling, beta_coupling, tile, *tiles]
    smem, vmem = pl.BlockSpec(memory_space=pltpu.SMEM), pl.BlockSpec(memory_space=pltpu.VMEM)

    def kernel(*refs):
        apply_kernel(alpha_slots, beta_slots, *refs)

    return pl.pallas_call(
        kernel,
        out_shape=jax.ShapeDtypeStruct(tile.shape, F32),
        in_specs=[smem] * 3 + [vmem] * 2 + [pl.BlockSpec(memory_space=pl.ANY)] * len(big),
        out_specs=vmem,
        scratch_shapes=[pltpu.VMEM(v.shape, F32) for v in big]
        + [pltpu.SemaphoreType.DMA((len(big),))]
        + [pltpu.VMEM((n, alpha_slots * n), BF16)] * 2
        + [pltpu.VMEM((alpha_slots * n, n), BF16)] * 2,
        cost_estimate=pl.CostEstimate(flops=6 * 5 * n**3, bytes_accessed=4 * 12 * n * n, transcendentals=0),
        name="apply_operator",
    )(plan, alpha_mask, beta_mask, alpha_energy, beta_energy, *big)


def per_device(
    coefficients,
    alpha_coupling,
    beta_coupling,
    alpha_energy,
    beta_energy,
    alpha_bits,
    beta_bits,
    alpha_mask,
    beta_mask,
):
    alpha_slots, beta_slots = alpha_coupling.shape[0], beta_coupling.shape[0]
    alpha_sets, beta_sets = colex(levels("alpha"), alpha_slots), colex(levels("beta"), beta_slots)
    smem = pl.BlockSpec(memory_space=pltpu.SMEM)
    plan = pl.pallas_call(
        plan_kernel,
        out_shape=jax.ShapeDtypeStruct((8,), jnp.int32),
        in_specs=[smem] * 2,
        out_specs=smem,
        name="plan",
    )(alpha_bits, beta_bits)
    alpha_arm, beta_arm = plan[0], plan[1]

    def exchange(alpha_set, beta_set):
        moves = [("alpha", b) for b in alpha_set] + [("beta", b) for b in beta_set]

        def run(tile):
            moved = {m: swapped(tile, *m) for m in sorted(moves, key=RANK.get)}
            return tuple(moved[m] for m in moves)

        return run

    def nested(alpha_set):
        return lambda tile: lax.switch(beta_arm, [exchange(alpha_set, s) for s in beta_sets], tile)

    def step(tile):
        tiles = lax.switch(alpha_arm, [nested(s) for s in alpha_sets], tile)
        return apply_operator(
            plan,
            alpha_mask,
            beta_mask,
            alpha_energy[None, :],
            beta_energy[None, :],
            alpha_coupling,
            beta_coupling,
            tile,
            tiles,
        )

    sigma_vector = step(coefficients)
    sigma_squared = step(sigma_vector)
    return (sigma_vector, sigma_squared)


def solution(mesh):
    return jax.shard_map(
        per_device,
        mesh=mesh,
        in_specs=(
            P("alpha", "beta"),
            P(None, "alpha", None),
            P(None, "beta", None),
            P("alpha"),
            P("beta"),
            P(),
            P(),
            P("alpha", None),
            P("beta", None),
        ),
        out_specs=(P("alpha", "beta"), P("alpha", "beta")),
        check_vma=False,
    )
```

```python
import itertools

import jax
import jax.numpy as jnp
from jax import lax
from jax.experimental import pallas as pl
from jax.experimental.pallas import tpu as pltpu
from jax.sharding import PartitionSpec as P

F32, BF16 = jnp.float32, jnp.bfloat16
ALPHA_CHEAP = 3
FAR, HALF = 3, 2
BETA_RANK = [0, 3, 4, 1, 2]


def swapped(value, axis, stride):
    mask = 2**stride
    pairs = [(source, source ^ mask) for source in range(lax.axis_size(axis))]
    return lax.ppermute(value, axis, pairs)


def shifted(value, step):
    a, b = lax.axis_size("alpha"), lax.axis_size("beta")
    run = 2 ** (HALF + 1)
    pairs = []
    for i, j in itertools.product(range(a), range(b)):
        z = (i // (a // 2)) * run + j % run
        z = (z + step) % (2 * run)
        to = (z // run) * (a // 2) + i % (a // 2), j - j % run + z % run
        pairs.append((i * b + j, to[0] * b + to[1]))
    return lax.ppermute(value, ("alpha", "beta"), pairs)


def levels(axis):
    return lax.axis_size(axis).bit_length() - 1


def colex(count, slots):
    return sorted(itertools.combinations(range(count), slots), key=lambda s: s[::-1])


def plan_kernel(alpha_bits, beta_bits, arm, plan):
    a0, a1 = alpha_bits[0], alpha_bits[1]
    far = jnp.logical_or(a0 == FAR, a1 == FAR).astype(jnp.int32)
    plan[0] = a0
    plan[1] = a1
    b = [beta_bits[k] for k in range(3)]
    ranks = [sum((b[j] < b[k]).astype(jnp.int32) for j in range(3) if j != k) for k in range(3)]
    low = jnp.minimum(jnp.minimum(b[0], b[1]), b[2])
    high = jnp.maximum(jnp.maximum(b[0], b[1]), b[2])
    middle = b[0] + b[1] + b[2] - low - high
    which = (high * (high - 1) * (high - 2)) // 6 + (middle * (middle - 1)) // 2 + low
    arm[0] = 2 * which + far
    for place in range(3):
        plan[2 + place] = sum(jnp.where(ranks[k] == place, k, 0) for k in range(3))


def split(value):
    high = value.astype(BF16)
    return high, (value - high.astype(F32)).astype(BF16)


def apply_kernel(alpha_slots, beta_slots, *refs):
    plan, alpha_mask, beta_mask, alpha_energy, beta_energy = refs[:5]
    sources = refs[5:8]
    near = refs[8 : 8 + ALPHA_CHEAP]
    far = refs[8 + ALPHA_CHEAP : 10 + ALPHA_CHEAP]
    beta_sources = refs[10 + ALPHA_CHEAP : 10 + ALPHA_CHEAP + beta_slots]
    out = refs[10 + ALPHA_CHEAP + beta_slots]
    rest = refs[11 + ALPHA_CHEAP + beta_slots :]
    alpha_coupling, beta_coupling, tile, alpha_tiles, beta_tiles, sems, lhs_hi, lhs_lo, rhs_hi, rhs_lo = rest
    n = tile.shape[0]

    base = [
        pltpu.make_async_copy(s, d, sems.at[i])
        for i, (s, d) in enumerate(zip(sources, (alpha_coupling, beta_coupling, tile)))
    ]
    base[0].start()
    for k in range(alpha_slots):
        bit = plan[k]
        for j in range(ALPHA_CHEAP):

            @pl.when(bit == j)
            def _():
                pltpu.make_async_copy(near[j], alpha_tiles.at[k], sems.at[3 + k]).start()

        @pl.when(bit == FAR)
        def _():
            for h in range(2):
                half = alpha_tiles.at[k, pl.ds(h * (n // 2), n // 2), :]
                pltpu.make_async_copy(far[h], half, sems.at[3 + k]).start()

    base[2].start()
    base[1].start()
    beta_copies = [
        pltpu.make_async_copy(beta_sources[p], beta_tiles.at[p], sems.at[3 + alpha_slots + p]) for p in range(beta_slots)
    ]
    for copy in beta_copies:
        copy.start()

    base[0].wait()
    for k in range(alpha_slots):
        pltpu.make_async_copy(near[0], alpha_tiles.at[k], sems.at[3 + k]).wait()
        at = pl.ds(k * n, n)
        lhs_hi[:, at], lhs_lo[:, at] = split(alpha_coupling[k] * alpha_mask[0, k].astype(F32))
        rhs_hi[at, :], rhs_lo[at, :] = split(alpha_tiles[k])

    def product(left, right):
        return lax.dot_general(left, right, (((1,), (0,)), ((), ())), preferred_element_type=F32)

    total = product(lhs_hi[...], rhs_hi[...])
    total += product(lhs_hi[...], rhs_lo[...])
    total += product(lhs_lo[...], rhs_hi[...])

    base[2].wait()
    rows = jnp.transpose(jnp.broadcast_to(alpha_energy[...].reshape(1, n), (128, n)))
    rows = jnp.concatenate([rows] * (n // 128), axis=1)
    out[...] = total + (rows + beta_energy[...].reshape(1, n)) * tile[...]

    base[1].wait()

    def against(left, right):
        return lax.dot_general(left, right, (((1,), (1,)), ((), ())), preferred_element_type=F32)

    total = None
    for place in range(beta_slots):
        beta_copies[place].wait()
        slot = plan[alpha_slots + place]
        right_hi, right_lo = split(beta_coupling[slot] * beta_mask[0, slot].astype(F32))
        left_hi, left_lo = split(beta_tiles[place])
        part = against(left_hi, right_hi) + against(left_lo, right_hi) + against(left_hi, right_lo)
        total = part if total is None else total + part
    out[...] += total


def apply_operator(plan, alpha_mask, beta_mask, alpha_energy, beta_energy, alpha_coupling, beta_coupling, tile, tiles):
    alpha_slots, beta_slots = alpha_coupling.shape[0], beta_coupling.shape[0]
    n = tile.shape[0]
    big = [alpha_coupling, beta_coupling, tile, *tiles]
    smem, vmem = pl.BlockSpec(memory_space=pltpu.SMEM), pl.BlockSpec(memory_space=pltpu.VMEM)

    def kernel(*refs):
        apply_kernel(alpha_slots, beta_slots, *refs)

    return pl.pallas_call(
        kernel,
        out_shape=jax.ShapeDtypeStruct(tile.shape, F32),
        in_specs=[smem] * 3 + [vmem] * 2 + [pl.BlockSpec(memory_space=pl.ANY)] * len(big),
        out_specs=vmem,
        scratch_shapes=[
            pltpu.VMEM(alpha_coupling.shape, F32),
            pltpu.VMEM(beta_coupling.shape, F32),
            pltpu.VMEM(tile.shape, F32),
            pltpu.VMEM((alpha_slots, n, n), F32),
            pltpu.VMEM((beta_slots, n, n), F32),
            pltpu.SemaphoreType.DMA((3 + alpha_slots + beta_slots,)),
        ]
        + [pltpu.VMEM((n, alpha_slots * n), BF16)] * 2
        + [pltpu.VMEM((alpha_slots * n, n), BF16)] * 2,
        cost_estimate=pl.CostEstimate(flops=6 * 5 * n**3, bytes_accessed=4 * 12 * n * n, transcendentals=0),
        name="apply_operator",
    )(plan, alpha_mask, beta_mask, alpha_energy, beta_energy, *big)


def exchange(far, beta_set):
    def run(tile):
        half = tile.shape[0] // 2
        near = [swapped(tile, "alpha", b) for b in range(ALPHA_CHEAP)]
        beta = {b: swapped(tile, "beta", b) for b in sorted(beta_set, key=BETA_RANK.index) if not (far and b == HALF)}
        if not far:
            upper = lower = jnp.zeros_like(tile[:half])
        elif HALF in beta_set:
            step = 2**HALF
            below, above = shifted(tile, step), shifted(tile, -step)
            upper, lower = shifted(below[:half], step), shifted(above[half:], -step)
            beta[HALF] = jnp.where((lax.axis_index("beta") >> HALF) & 1 == 1, below, above)
        else:
            upper, lower = swapped(tile[:half], "alpha", FAR), swapped(tile[half:], "alpha", FAR)
        return (*near, upper, lower, *(beta[b] for b in beta_set))

    return run


def per_device(
    coefficients,
    alpha_coupling,
    beta_coupling,
    alpha_energy,
    beta_energy,
    alpha_bits,
    beta_bits,
    alpha_mask,
    beta_mask,
):
    smem = pl.BlockSpec(memory_space=pltpu.SMEM)
    arm, plan = pl.pallas_call(
        plan_kernel,
        out_shape=(jax.ShapeDtypeStruct((1,), jnp.int32), jax.ShapeDtypeStruct((8,), jnp.int32)),
        in_specs=[smem] * 2,
        out_specs=(smem, smem),
        name="plan",
    )(alpha_bits, beta_bits)
    arms = [exchange(far, s) for s in colex(levels("beta"), beta_coupling.shape[0]) for far in (False, True)]

    def body(_, fields):
        tile, _ = fields
        tiles = lax.switch(arm[0], arms, tile)
        image = apply_operator(
            plan, alpha_mask, beta_mask, alpha_energy, beta_energy, alpha_coupling, beta_coupling, tile, tiles
        )
        return image, tile

    sigma_squared, sigma_vector = lax.fori_loop(0, 2, body, (coefficients, coefficients))
    return (sigma_vector, sigma_squared)


def solution(mesh):
    return jax.shard_map(
        per_device,
        mesh=mesh,
        in_specs=(
            P("alpha", "beta"),
            P(None, "alpha", None),
            P(None, "beta", None),
            P("alpha"),
            P("beta"),
            P(),
            P(),
            P("alpha", None),
            P("beta", None),
        ),
        out_specs=(P("alpha", "beta"), P("alpha", "beta")),
        check_vma=False,
    )
```
